512 devices in a mesh: section: 4 (over x), seq: 16 (over y, z_lo), wide: 8 (over z_hi, core).
Axes of the slice: x: 4, y: 4, z: 16 (z_hi: 4, z_lo: 4; z = z_hi * 4 + z_lo), core: 2. Of those that a mesh axis runs over, the one named last changes fastest.
Arguments:
- q_self: bfloat16 [4, 4096, 5120], P('section', 'seq', 'wide'), may hold values from -6 to 6
- k_self: bfloat16 [4, 4096, 5120], P('section', 'seq', 'wide'), may hold values from -6 to 6
- v_self: bfloat16 [4, 4096, 5120], P('section', 'seq', 'wide'), may hold values from -6 to 6
- gain_q_self: float32 [5120], P('wide'), may hold values from 1.2 to 2.4
- gain_k_self: float32 [5120], P('wide'), may hold values from 1.2 to 2.4
- counts: int32 [4], replicated, may hold values from 1 to 4096, 12288 in all
- q_cross: bfloat16 [4, 4096, 5120], P('section', 'seq', 'wide'), may hold values from -6 to 6
- cap_kv: bfloat16 [2, 4, 512, 5120], P(None, 'section', 'seq', 'wide'), may hold values from -6 to 6
- gain_q_cross: float32 [5120], P('wide'), may hold values from 1.2 to 2.4
- gain_k_cross: float32 [5120], P('wide'), may hold values from 1.2 to 2.4
- cap_len: int32 [4], replicated, may hold values from 1 to 512, 1024 in all
- owner: int32 [4], replicated, may hold values from 0 to 3, each once
Outputs:
- out_self: bfloat16 [4, 4096, 5120], P('section', 'seq', 'wide')
- out_cross: bfloat16 [4, 4096, 5120], P('section', 'seq', 'wide')
The draws below stay inside these ranges and needn't reach their ends.
Inputs may be any that keep to these rules, and one draw needn't show every extreme that they name: owner is a permutation of the clips.
All inputs are finite; a program needn't handle non-finite values.
Results may differ from the reference program's by a relative error of at most 0.012.
The reference program's roundings to bfloat16 on the way count: a program that leaves them out, or rounds other values in their place, can miss the bound.
Values may be sent and summed in bfloat16 or wider, within the bound.
A program may use at most 128 MiB of HBM per device.

```python
import math
import jax
import jax.numpy as jnp
import numpy as np
from jax import lax

D = 5120
HEADS = 40
HEAD = 128
CAP = 512
CLIPS = 4
L = 4096


def drawn_pair(key, rows, keys_rows, keys_groups):
    first = jax.random.fold_in(key, 101)
    second = jax.random.fold_in(key, 102)
    queries = jax.random.normal(first, (CLIPS, rows, D), jnp.float32)
    keys = jax.random.normal(second, (keys_groups, keys_rows, D), jnp.float32)
    return (jnp.clip(queries, -6.0, 6.0), jnp.clip(keys, -6.0, 6.0))


def draw_q_self(key, part):
    return drawn_pair(key, L, L, CLIPS)[0].astype(jnp.bfloat16)


def draw_k_self(key, part):
    return drawn_pair(key, L, L, CLIPS)[1].astype(jnp.bfloat16)


def draw_q_cross(key, part):
    return drawn_pair(jax.random.fold_in(key, 7), L, CAP, CLIPS + 0 * L + 0)[0].astype(jnp.bfloat16) if CAP != L else cross_pair(key)[0]


def cross_pair(key):
    inner = jax.random.fold_in(key, 7)
    queries = jax.random.normal(jax.random.fold_in(inner, 101), (CLIPS, L, D), jnp.float32)
    keys = jax.random.normal(jax.random.fold_in(inner, 102), (CLIPS, CAP, D), jnp.float32)
    return (jnp.clip(queries, -6.0, 6.0).astype(jnp.bfloat16), jnp.clip(keys, -6.0, 6.0))


def draw_cap_kv(key, part):
    keys = cross_pair(key)[1]
    values = jax.random.normal(jax.random.fold_in(key, 205), (CLIPS, CAP, D), jnp.float32)
    return jnp.stack([keys, jnp.clip(values, -6.0, 6.0)]).astype(jnp.bfloat16)


def block_levels(key, extent, cuts, least, high):
    loudness = 1.0
    for position, shards_of in cuts:
        heights = jax.random.uniform(jax.random.fold_in(jax.random.fold_in(key, 6), position), (shards_of,), jnp.float32, least / len(cuts), high / len(cuts))
        loudness = loudness * jnp.repeat(jnp.exp(heights), extent[position] // shards_of).reshape((-1,) + (1,) * (len(extent) - 1 - position))
    return loudness


def length_profile(amount, total, reach, slope):
    loads = [(1 << 20) // math.isqrt(rank ** slope) + 1 for rank in range(2, amount + 1)]
    spare, holding = total - reach - (amount - 1), [1] * (amount - 1)
    while spare > 0:
        free = [i for i in range(amount - 1) if holding[i] < reach]
        mass, budget = sum([loads[i] for i in free]), spare
        for i in free:
            extra = min(reach - holding[i], max(1, budget * loads[i] // mass), spare)
            holding[i] = holding[i] + extra
            spare = spare - extra
    return np.array([reach] + holding)


def uneven(key, number_of, total, reach, skew):
    if number_of == 2:
        one = jax.random.randint(key, (), max(1, total - reach), min(reach, total - 1) + 1)
        return jnp.stack([one, total - one])
    lengths = jnp.asarray(length_profile(number_of, total, reach, skew), jnp.int32)
    couples = (number_of - 1) // 2
    giver, taker = lengths[1:1 + 2 * couples:2], lengths[2:2 + 2 * couples:2]
    room = jnp.minimum(giver - 1, reach - taker)
    shifted = jax.random.randint(jax.random.fold_in(key, 1), (couples,), 0, 1 << 20) % (room + 1)
    lengths = lengths.at[1:1 + 2 * couples:2].set(giver - shifted).at[2:2 + 2 * couples:2].set(taker + shifted)
    return lengths[jax.random.permutation(jax.random.fold_in(key, 2), number_of)]


def gaussian(key, extent, spread, reach, split=(), held_as=jnp.bfloat16):
    level = block_levels(key, extent, split, -0.22, 0.18) if split else 1.0
    entries = jax.random.normal(key, extent, jnp.float32) * spread * level
    return jnp.minimum(jnp.maximum(entries, -reach), reach).astype(held_as)


def setup_inputs(seed: int = 0) -> dict:
    arg_keys = jax.random.split(jax.random.key(seed), 13)
    return {
        "q_self": draw_q_self(jax.random.fold_in(arg_keys[12], 71), 0),
        "k_self": draw_k_self(jax.random.fold_in(arg_keys[12], 71), 0),
        "v_self": gaussian(arg_keys[2], (CLIPS, L, D), 1.0, 6.0, ((0, 4), (1, 16), (2, 8))),
        "gain_q_self": jnp.clip(1.2 + 1.2 * jax.random.uniform(arg_keys[3], (D,), jnp.float32) ** block_levels(arg_keys[3], (D,), ((0, 8),), -0.2, 0.2), 1.2, 2.4),
        "gain_k_self": jnp.clip(1.2 + 1.2 * jax.random.uniform(arg_keys[4], (D,), jnp.float32) ** block_levels(arg_keys[4], (D,), ((0, 8),), -0.2, 0.2), 1.2, 2.4),
        "counts": uneven(arg_keys[5], CLIPS, 3 * L, L, 2).astype(jnp.int32),
        "q_cross": draw_q_cross(jax.random.fold_in(arg_keys[12], 71), 0),
        "cap_kv": draw_cap_kv(jax.random.fold_in(arg_keys[12], 71), 0),
        "gain_q_cross": jnp.clip(1.2 + 1.2 * jax.random.uniform(arg_keys[8], (D,), jnp.float32) ** block_levels(arg_keys[8], (D,), ((0, 8),), -0.2, 0.2), 1.2, 2.4),
        "gain_k_cross": jnp.clip(1.2 + 1.2 * jax.random.uniform(arg_keys[9], (D,), jnp.float32) ** block_levels(arg_keys[9], (D,), ((0, 8),), -0.2, 0.2), 1.2, 2.4),
        "cap_len": uneven(arg_keys[10], CLIPS, 2 * CAP, CAP, 2).astype(jnp.int32),
        "owner": jax.random.permutation(arg_keys[11], CLIPS).astype(jnp.int32),
    }


def normalized(values, gain):
    floats = values.astype(jnp.float32)
    mean_square = lax.optimization_barrier(jnp.mean(floats * floats, axis=-1, keepdims=True))
    return (floats * lax.rsqrt(mean_square + 1e-06) * gain.astype(jnp.float32)).astype(jnp.bfloat16)

def one_head(queries, keys, values, valid):
    scores = jnp.dot(queries, keys.T, preferred_element_type=jnp.float32) / math.sqrt(HEAD)
    scores = jnp.where(valid[None, :], scores, -jnp.inf)
    top = lax.optimization_barrier(jnp.max(scores, axis=-1, keepdims=True))
    expo = jnp.exp(scores - top)
    total = lax.optimization_barrier(jnp.sum(expo, axis=-1, keepdims=True))
    weights = expo.astype(jnp.bfloat16)
    return (jnp.dot(weights, values, preferred_element_type=jnp.float32) / total).astype(jnp.bfloat16)

def attention(queries, keys, values, valid):
    split_q = queries.reshape(-1, HEADS, HEAD).transpose(1, 0, 2)
    split_k = keys.reshape(-1, HEADS, HEAD).transpose(1, 0, 2)
    split_v = values.reshape(-1, HEADS, HEAD).transpose(1, 0, 2)
    result = lax.map(lambda trio: one_head(trio[0], trio[1], trio[2], valid), (split_q, split_k, split_v))
    return result.transpose(1, 0, 2).reshape(-1, D)

def reference(q_self, k_self, v_self, gain_q_self, gain_k_self, counts, q_cross, cap_kv, gain_q_cross, gain_k_cross, cap_len, owner):
    self_list = []
    cross_list = []
    index = jnp.arange(CLIPS, dtype=jnp.int32)
    for clip in range(CLIPS):
        q_hat = normalized(q_self[clip], gain_q_self)
        k_hat = normalized(k_self[clip], gain_k_self)
        valid = jnp.arange(L, dtype=jnp.int32) < counts[clip]
        self_list.append(attention(q_hat, k_hat, v_self[clip], valid))
        source = jnp.sum(jnp.where(owner == clip, index, 0)).astype(jnp.int32)
        caption = cap_kv[:, source]
        caption_keys = normalized(caption[0], gain_k_cross)
        cross_hat = normalized(q_cross[clip], gain_q_cross)
        live = jnp.arange(CAP, dtype=jnp.int32) < cap_len[source]
        cross_list.append(attention(cross_hat, caption_keys, caption[1], live))
    return (jnp.stack(self_list), jnp.stack(cross_list))
```

```python
import functools
import math

import jax
import jax.numpy as jnp
from jax import lax
from jax.experimental import pallas as pl
from jax.experimental.pallas import tpu as pltpu
from jax.sharding import PartitionSpec as P

D = 5120
HEAD = 128
MESH = pl.DeviceIdType.MESH
MASKED = -1e30
PER_HEAD = 3
STEP = 80
PIECE = 96
EXTRA = PIECE - STEP


def square_sums(values):
    floats = values.astype(jnp.float32)
    return jnp.sum(floats * floats, axis=-1)


def scaled_rows(values, total_squares, gain):
    floats = values.astype(jnp.float32)
    factor = lax.rsqrt(total_squares / D + 1e-06)
    return (floats * factor[:, None] * gain[None, :]).astype(jnp.bfloat16)


def attend(q, key_ref, value_ref, bias_ref, slots):
    total_slots, rows, _ = key_ref.shape
    block = slots * rows
    scale = math.log2(math.e) / math.sqrt(HEAD)

    def body(number, carry):
        top, total, accum = carry
        keys = key_ref[pl.ds(number * slots, slots)].reshape(block, HEAD)
        values = value_ref[pl.ds(number * slots, slots)].reshape(block, HEAD)
        scores = lax.dot_general(
            q, keys, (((1,), (1,)), ((), ())), preferred_element_type=jnp.float32
        )
        start = pl.multiple_of(number * block, 128)
        scores = scores + bias_ref[0:1, pl.ds(start, block)]
        newest = jnp.maximum(top, jnp.max(scores, axis=-1, keepdims=True))
        weights = jnp.exp2((scores - newest) * scale)
        rescale = jnp.exp2((top - newest) * scale)
        total = total * rescale + jnp.sum(weights, axis=-1, keepdims=True)
        accum = accum * rescale + jnp.dot(
            weights.astype(jnp.bfloat16), values, preferred_element_type=jnp.float32
        )
        return (newest, total, accum)

    count = q.shape[0]
    state = (
        jnp.full((count, 1), MASKED, jnp.float32),
        jnp.zeros((count, 1), jnp.float32),
        jnp.zeros((count, HEAD), jnp.float32),
    )
    top, total, accum = lax.fori_loop(0, total_slots // slots, body, state)
    return (accum / total).astype(jnp.bfloat16)


def main_kernel(
    n, heads_here,
    limits, q, k, v, cq, ck, cv,
    out_self, out_cross,
    kr, vr, qr, ckr, cvr, cqr, os_buf, oc_buf, bias, cbias,
    send, recv, local, osend, orecv, olocal,
):
    me = lax.axis_index("seq")
    owners = heads_here * PER_HEAD
    barrier = pltpu.get_barrier_semaphore()

    @pl.loop(1, n)
    def _(d):
        pl.semaphore_signal(
            barrier, inc=1, device_id={"seq": lax.rem(me + d, n)}, device_id_type=MESH
        )

    pl.semaphore_wait(barrier, n - 1)

    def pieces(target):
        columns = pl.ds(pl.multiple_of((target // PER_HEAD) * HEAD, HEAD), HEAD)
        part = pl.ds(pl.multiple_of((target % PER_HEAD) * STEP, 16), PIECE)
        return (
            (k.at[:, columns], kr),
            (v.at[:, columns], vr),
            (q.at[part, columns], qr),
            (ck.at[:, columns], ckr),
            (cv.at[:, columns], cvr),
            (cq.at[part, columns], cqr),
        )

    def copies(d):
        target = lax.rem(me + d, n)
        return [
            pltpu.make_async_remote_copy(
                source, landing.at[me], send.at[d, number], recv.at[d, number],
                device_id={"seq": target}, device_id_type=MESH,
            )
            for number, (source, landing) in enumerate(pieces(target))
        ]

    def own_copies():
        return [
            pltpu.make_async_copy(source, landing.at[me], local.at[number])
            for number, (source, landing) in enumerate(pieces(me))
        ]

    @pl.loop(1, n)
    def _(d):
        @pl.when(lax.rem(me + d, n) < owners)
        def _():
            for copy in copies(d):
                copy.start()

    @pl.when(me < owners)
    def _():
        for copy in own_copies():
            copy.start()

    position = lax.broadcasted_iota(jnp.int32, bias.shape, 1)
    bias[...] = jnp.where(position < limits[0], 0.0, MASKED)
    position = lax.broadcasted_iota(jnp.int32, cbias.shape, 1)
    cbias[...] = jnp.where(position < limits[1], 0.0, MASKED)

    def arrivals(d):
        for number, landing in enumerate((kr, vr, qr, ckr, cvr, cqr)):
            pltpu.make_async_remote_copy(
                landing.at[0], landing.at[0], send.at[d, number], recv.at[d, number],
                device_id={"seq": lax.rem(me + 1, n)}, device_id_type=MESH,
            ).wait_recv()

    columns = pl.ds(pl.multiple_of((me // PER_HEAD) * HEAD, HEAD), HEAD)
    third = me % PER_HEAD

    def results(d, to, make):
        rows = pl.ds(pl.multiple_of(third * STEP + EXTRA, 16), STEP)
        found = []
        for number, (buf, out) in enumerate(((os_buf, out_self), (oc_buf, out_cross))):
            found.append(
                make(buf.at[to, pl.ds(EXTRA, STEP)], out.at[rows, columns], d, 2 * number)
            )
        return found

    def first_rows(d, to, make):
        found = []
        for number, (buf, out) in enumerate(((os_buf, out_self), (oc_buf, out_cross))):
            found.append(
                make(buf.at[to, pl.ds(0, EXTRA)], out.at[pl.ds(0, EXTRA), columns], d, 2 * number + 1)
            )
        return found

    def remote(source, landing, d, number):
        return pltpu.make_async_remote_copy(
            source, landing, osend.at[d, number], orecv.at[d, number],
            device_id={"seq": lax.rem(me + d, n)}, device_id_type=MESH,
        )

    def nearby(source, landing, d, number):
        return pltpu.make_async_copy(source, landing, olocal.at[number])

    @pl.when(me < owners)
    def _():
        for copy in own_copies():
            copy.wait()

        @pl.loop(1, n)
        def _(d):
            arrivals(d)

        group = 4
        @pl.loop(0, n // group)
        def _(g):
            queries = qr[pl.ds(g * group, group)].reshape(group * PIECE, HEAD)
            os_buf[pl.ds(g * group, group)] = attend(queries, kr, vr, bias, 4).reshape(
                group, PIECE, HEAD
            )
            queries = cqr[pl.ds(g * group, group)].reshape(group * PIECE, HEAD)
            oc_buf[pl.ds(g * group, group)] = attend(queries, ckr, cvr, cbias, 16).reshape(
                group, PIECE, HEAD
            )

        @pl.loop(1, n)
        def _(d):
            for copy in results(d, lax.rem(me + d, n), remote):
                copy.start()

            @pl.when(third == 0)
            def _():
                for copy in first_rows(d, lax.rem(me + d, n), remote):
                    copy.start()

        for copy in results(0, me, nearby):
            copy.start()

        @pl.when(third == 0)
        def _():
            for copy in first_rows(0, me, nearby):
                copy.start()

    @pl.loop(1, n)
    def _(d):
        @pl.when(lax.rem(me + d, n) < owners)
        def _():
            for copy in copies(d):
                copy.wait_send()

        sender = lax.rem(me + n - d, n)
        for number, out in ((0, out_self), (2, out_cross)):
            @pl.when(sender < owners)
            def _():
                piece = out.at[pl.ds(0, STEP), pl.ds(0, HEAD)]
                remote(piece, piece, d, number).wait_recv()

            @pl.when((sender < owners) & (sender % PER_HEAD == 0))
            def _():
                piece = out.at[pl.ds(0, EXTRA), pl.ds(0, HEAD)]
                remote(piece, piece, d, number + 1).wait_recv()

    @pl.when(me < owners)
    def _():
        for copy in results(0, me, nearby):
            copy.wait()

        @pl.when(third == 0)
        def _():
            for copy in first_rows(0, me, nearby):
                copy.wait()

        @pl.loop(1, n)
        def _(d):
            for copy in results(d, lax.rem(me + d, n), remote):
                copy.wait_send()

            @pl.when(third == 0)
            def _():
                for copy in first_rows(d, lax.rem(me + d, n), remote):
                    copy.wait_send()


def exchange_and_attend(limits, q, k, v, cq, ck, cv):
    n = lax.axis_size("seq")
    rows, width = q.shape
    cap_rows = ck.shape[0]
    bf16 = jnp.bfloat16
    vmem = pl.BlockSpec(memory_space=pltpu.VMEM)
    return pl.pallas_call(
        functools.partial(main_kernel, n, width // HEAD),
        out_shape=(
            jax.ShapeDtypeStruct((rows, width), bf16),
            jax.ShapeDtypeStruct((rows, width), bf16),
        ),
        in_specs=[pl.BlockSpec(memory_space=pltpu.SMEM)] + [vmem] * 6,
        out_specs=(vmem, vmem),
        scratch_shapes=[
            pltpu.VMEM((n, rows, HEAD), bf16),
            pltpu.VMEM((n, rows, HEAD), bf16),
            pltpu.VMEM((n, PIECE, HEAD), bf16),
            pltpu.VMEM((n, cap_rows, HEAD), bf16),
            pltpu.VMEM((n, cap_rows, HEAD), bf16),
            pltpu.VMEM((n, PIECE, HEAD), bf16),
            pltpu.VMEM((n, PIECE, HEAD), bf16),
            pltpu.VMEM((n, PIECE, HEAD), bf16),
            pltpu.VMEM((8, n * rows), jnp.float32),
            pltpu.VMEM((8, n * cap_rows), jnp.float32),
            pltpu.SemaphoreType.DMA((n, 6)),
            pltpu.SemaphoreType.DMA((n, 6)),
            pltpu.SemaphoreType.DMA((6,)),
            pltpu.SemaphoreType.DMA((n, 4)),
            pltpu.SemaphoreType.DMA((n, 4)),
            pltpu.SemaphoreType.DMA((4,)),
        ],
        compiler_params=pltpu.CompilerParams(
            collective_id=0, has_side_effects=True, vmem_limit_bytes=56 << 20
        ),
    )(limits, q, k, v, cq, ck, cv)


def per_device(
    q_self,
    k_self,
    v_self,
    gain_q_self,
    gain_k_self,
    counts,
    q_cross,
    cap_kv,
    gain_q_cross,
    gain_k_cross,
    cap_len,
    owner,
):
    section = lax.axis_index("section")
    numbers = jnp.arange(lax.axis_size("section"), dtype=jnp.int32)
    source = jnp.sum(jnp.where(owner == section, numbers, 0))
    limits = jnp.stack([counts[section], cap_len[source]])
    captions = lax.all_gather(cap_kv, "section", axis=1, tiled=True)
    caption = lax.dynamic_index_in_dim(captions, source, 1, keepdims=False)
    totals = lax.psum(
        (
            square_sums(q_self[0]),
            square_sums(k_self[0]),
            square_sums(q_cross[0]),
            square_sums(caption[0]),
        ),
        "wide",
    )
    out_self, out_cross = exchange_and_attend(
        limits,
        scaled_rows(q_self[0], totals[0], gain_q_self),
        scaled_rows(k_self[0], totals[1], gain_k_self),
        v_self[0],
        scaled_rows(q_cross[0], totals[2], gain_q_cross),
        scaled_rows(caption[0], totals[3], gain_k_cross),
        caption[1],
    )
    return (out_self[None], out_cross[None])


def solution(mesh):
    whole = P("section", "seq", "wide")
    return jax.shard_map(
        per_device,
        mesh=mesh,
        in_specs=(
            whole, whole, whole, P("wide"), P("wide"), P(), whole,
            P(None, "section", "seq", "wide"), P("wide"), P("wide"), P(), P(),
        ),
        out_specs=(whole, whole),
        check_vma=False,
    )
```

```python
import functools
import math

import jax
import jax.numpy as jnp
from jax import lax
from jax.experimental import pallas as pl
from jax.experimental.pallas import tpu as pltpu
from jax.sharding import PartitionSpec as P

D = 5120
HEAD = 128
MESH = pl.DeviceIdType.MESH
MASKED = -1e30
PER_HEAD = 3
STEP = 80
PIECE = 96
EXTRA = PIECE - STEP


def square_sums(ref):
    floats = ref.astype(jnp.float32)
    return jnp.sum(floats * floats, axis=-1, keepdims=True)


def scaled_rows(values, factor, gain):
    return (values.astype(jnp.float32) * factor * gain).astype(jnp.bfloat16)


def attend(q, key_ref, value_ref, bias_ref, slots):
    total_slots, rows, _ = key_ref.shape
    block = slots * rows
    scale = math.log2(math.e) / math.sqrt(HEAD)

    def body(number, carry):
        top, total, accum = carry
        keys = key_ref[pl.ds(number * slots, slots)].reshape(block, HEAD)
        values = value_ref[pl.ds(number * slots, slots)].reshape(block, HEAD)
        scores = lax.dot_general(
            q, keys, (((1,), (1,)), ((), ())), preferred_element_type=jnp.float32
        )
        start = pl.multiple_of(number * block, 128)
        scores = scores + bias_ref[0:1, pl.ds(start, block)]
        newest = jnp.maximum(top, jnp.max(scores, axis=-1, keepdims=True))
        weights = jnp.exp2((scores - newest) * scale)
        rescale = jnp.exp2((top - newest) * scale)
        total = total * rescale + jnp.sum(weights, axis=-1, keepdims=True)
        accum = accum * rescale + jnp.dot(
            weights.astype(jnp.bfloat16), values, preferred_element_type=jnp.float32
        )
        return (newest, total, accum)

    count = q.shape[0]
    state = (
        jnp.full((count, 1), MASKED, jnp.float32),
        jnp.zeros((count, 1), jnp.float32),
        jnp.zeros((count, HEAD), jnp.float32),
    )
    top, total, accum = lax.fori_loop(0, total_slots // slots, body, state)
    return (accum / total).astype(jnp.bfloat16)


def main_kernel(
    n, sections, wides, heads_here,
    counts, cap_len, owner, q_raw, k_raw, v, cq_raw, cap, gq, gk, gcq, gck,
    out_self, out_cross,
    kr, vr, qr, ckr, cvr, cqr, os_buf, oc_buf, bias, cbias,
    q, k, cq, capr, chosen, columns_of, stat, stats, factors,
    send, recv, local, osend, orecv, olocal, wsend, wrecv, ssend, srecv,
):
    me = lax.axis_index("seq")
    section = lax.axis_index("section")
    wide = lax.axis_index("wide")
    owners = heads_here * PER_HEAD
    barrier = pltpu.get_barrier_semaphore()
    for axis, here, size in (("seq", me, n), ("section", section, sections), ("wide", wide, wides)):
        @pl.loop(1, size)
        def _(d):
            pl.semaphore_signal(
                barrier, inc=1, device_id={axis: lax.rem(here + d, size)}, device_id_type=MESH
            )

    pl.semaphore_wait(barrier, n + sections + wides - 3)
    ck, cv = chosen.at[0], chosen.at[1]

    def pieces(target):
        columns = pl.ds(pl.multiple_of((target // PER_HEAD) * HEAD, HEAD), HEAD)
        part = pl.ds(pl.multiple_of((target % PER_HEAD) * STEP, 16), PIECE)
        return (
            (k.at[:, columns], kr),
            (v.at[:, columns], vr),
            (q.at[part, columns], qr),
            (ck.at[:, columns], ckr),
            (cv.at[:, columns], cvr),
            (cq.at[part, columns], cqr),
        )

    def copies(d, numbers=range(6)):
        target = lax.rem(me + d, n)
        return [
            pltpu.make_async_remote_copy(
                source, landing.at[me], send.at[d, number], recv.at[d, number],
                device_id={"seq": target}, device_id_type=MESH,
            )
            for number, (source, landing) in enumerate(pieces(target)) if number in numbers
        ]

    def own_copies(numbers=range(6)):
        return [
            pltpu.make_async_copy(source, landing.at[me], local.at[number])
            for number, (source, landing) in enumerate(pieces(me)) if number in numbers
        ]

    def start(numbers):
        @pl.loop(1, n)
        def _(d):
            @pl.when(lax.rem(me + d, n) < owners)
            def _():
                for copy in copies(d, numbers):
                    copy.start()

        @pl.when(me < owners)
        def _():
            for copy in own_copies(numbers):
                copy.start()

    def to_section(d, number):
        return pltpu.make_async_remote_copy(
            (cap if number == 1 else capr.at[section]).at[number],
            capr.at[section, number], ssend.at[d, number], srecv.at[d, number],
            device_id={"section": lax.rem(section + d, sections)}, device_id_type=MESH,
        )

    def to_wide(d):
        return pltpu.make_async_remote_copy(
            stat, stats.at[wide], wsend.at[d], wrecv.at[d],
            device_id={"wide": lax.rem(wide + d, wides)}, device_id_type=MESH,
        )

    cap_rows = cap.shape[1]
    lane = lax.broadcasted_iota(jnp.int32, columns_of.shape, 1)
    columns_of[...] = jnp.where(
        lane == 0, square_sums(q_raw[...]),
        jnp.where(lane == 1, square_sums(k_raw[...]),
                  jnp.where(lane == 2, square_sums(cq_raw[...]), 0.0)),
    )
    columns_of[0:cap_rows] = jnp.where(
        lane[0:cap_rows] == 3, square_sums(cap[0]), columns_of[0:cap_rows]
    )
    partial = columns_of[...].T[0:8]
    stat[...] = partial
    stats[wide] = partial
    capr[section, 1] = cap[1]
    factors[...] = jnp.zeros(factors.shape, jnp.float32)

    @pl.loop(1, wides)
    def _(d):
        to_wide(d).start()

    start((1,))
    for d in range(1, sections):
        to_section(d, 1).start()

    source = section * 0
    for s in range(sections):
        source = jnp.where(owner[s] == section, s, source)
    position = lax.broadcasted_iota(jnp.int32, bias.shape, 1)
    bias[...] = jnp.where(position < counts[section], 0.0, MASKED)
    position = lax.broadcasted_iota(jnp.int32, cbias.shape, 1)
    cbias[...] = jnp.where(position < cap_len[source], 0.0, MASKED)

    @pl.loop(1, wides)
    def _(d):
        to_wide(d).wait_recv()

    total = stats[0]
    for w in range(1, wides):
        total = total + stats[w]
    factors[0:8] = lax.rsqrt(total / D + 1e-06)
    factor = factors[...].T
    capr[section, 0] = scaled_rows(cap[0], factor[0:cap_rows, 3:4], gck[...])
    k[...] = scaled_rows(k_raw[...], factor[:, 1:2], gk[...])
    q[...] = scaled_rows(q_raw[...], factor[:, 0:1], gq[...])
    cq[...] = scaled_rows(cq_raw[...], factor[:, 2:3], gcq[...])
    for d in range(1, sections):
        to_section(d, 0).start()
    start((0,))
    start((2, 5))
    for d in range(1, sections):
        for number in range(2):
            to_section(d, number).wait_recv()
    chosen[...] = capr[source]
    start((3, 4))

    def arrivals(d):
        for number, landing in enumerate((kr, vr, qr, ckr, cvr, cqr)):
            pltpu.make_async_remote_copy(
                landing.at[0], landing.at[0], send.at[d, number], recv.at[d, number],
                device_id={"seq": lax.rem(me + 1, n)}, device_id_type=MESH,
            ).wait_recv()

    columns = pl.ds(pl.multiple_of((me // PER_HEAD) * HEAD, HEAD), HEAD)
    third = me % PER_HEAD

    def results(d, to, make):
        rows = pl.ds(pl.multiple_of(third * STEP + EXTRA, 16), STEP)
        found = []
        for number, (buf, out) in enumerate(((os_buf, out_self), (oc_buf, out_cross))):
            found.append(
                make(buf.at[to, pl.ds(EXTRA, STEP)], out.at[rows, columns], d, 2 * number)
            )
        return found

    def first_rows(d, to, make):
        found = []
        for number, (buf, out) in enumerate(((os_buf, out_self), (oc_buf, out_cross))):
            found.append(
                make(buf.at[to, pl.ds(0, EXTRA)], out.at[pl.ds(0, EXTRA), columns], d, 2 * number + 1)
            )
        return found

    def remote(source, landing, d, number):
        return pltpu.make_async_remote_copy(
            source, landing, osend.at[d, number], orecv.at[d, number],
            device_id={"seq": lax.rem(me + d, n)}, device_id_type=MESH,
        )

    def nearby(source, landing, d, number):
        return pltpu.make_async_copy(source, landing, olocal.at[number])

    @pl.when(me < owners)
    def _():
        for copy in own_copies():
            copy.wait()

        @pl.loop(1, n)
        def _(d):
            arrivals(d)

        group = 4
        @pl.loop(0, n // group)
        def _(g):
            queries = qr[pl.ds(g * group, group)].reshape(group * PIECE, HEAD)
            os_buf[pl.ds(g * group, group)] = attend(queries, kr, vr, bias, 4).reshape(
                group, PIECE, HEAD
            )
            queries = cqr[pl.ds(g * group, group)].reshape(group * PIECE, HEAD)
            oc_buf[pl.ds(g * group, group)] = attend(queries, ckr, cvr, cbias, 16).reshape(
                group, PIECE, HEAD
            )

        @pl.loop(1, n)
        def _(d):
            for copy in results(d, lax.rem(me + d, n), remote):
                copy.start()

            @pl.when(third == 0)
            def _():
                for copy in first_rows(d, lax.rem(me + d, n), remote):
                    copy.start()

        for copy in results(0, me, nearby):
            copy.start()

        @pl.when(third == 0)
        def _():
            for copy in first_rows(0, me, nearby):
                copy.start()

    @pl.loop(1, n)
    def _(d):
        @pl.when(lax.rem(me + d, n) < owners)
        def _():
            for copy in copies(d):
                copy.wait_send()

        sender = lax.rem(me + n - d, n)
        for number, out in ((0, out_self), (2, out_cross)):
            @pl.when(sender < owners)
            def _():
                piece = out.at[pl.ds(0, STEP), pl.ds(0, HEAD)]
                remote(piece, piece, d, number).wait_recv()

            @pl.when((sender < owners) & (sender % PER_HEAD == 0))
            def _():
                piece = out.at[pl.ds(0, EXTRA), pl.ds(0, HEAD)]
                remote(piece, piece, d, number + 1).wait_recv()

    @pl.loop(1, wides)
    def _(d):
        to_wide(d).wait_send()

    for d in range(1, sections):
        for number in range(2):
            to_section(d, number).wait_send()

    @pl.when(me < owners)
    def _():
        for copy in results(0, me, nearby):
            copy.wait()

        @pl.when(third == 0)
        def _():
            for copy in first_rows(0, me, nearby):
                copy.wait()

        @pl.loop(1, n)
        def _(d):
            for copy in results(d, lax.rem(me + d, n), remote):
                copy.wait_send()

            @pl.when(third == 0)
            def _():
                for copy in first_rows(d, lax.rem(me + d, n), remote):
                    copy.wait_send()


def exchange_and_attend(counts, cap_len, owner, q, k, v, cq, cap, gq, gk, gcq, gck):
    n, sections, wides = (lax.axis_size(axis) for axis in ("seq", "section", "wide"))
    rows, width = q.shape
    cap_rows = cap.shape[1]
    bf16, f32 = jnp.bfloat16, jnp.float32
    vmem = pl.BlockSpec(memory_space=pltpu.VMEM)
    dma = pltpu.SemaphoreType.DMA
    return pl.pallas_call(
        functools.partial(main_kernel, n, sections, wides, width // HEAD),
        out_shape=(
            jax.ShapeDtypeStruct((rows, width), bf16),
            jax.ShapeDtypeStruct((rows, width), bf16),
        ),
        in_specs=[pl.BlockSpec(memory_space=pltpu.SMEM)] * 3 + [vmem] * 9,
        out_specs=(vmem, vmem),
        scratch_shapes=[
            pltpu.VMEM((n, rows, HEAD), bf16),
            pltpu.VMEM((n, rows, HEAD), bf16),
            pltpu.VMEM((n, PIECE, HEAD), bf16),
            pltpu.VMEM((n, cap_rows, HEAD), bf16),
            pltpu.VMEM((n, cap_rows, HEAD), bf16),
            pltpu.VMEM((n, PIECE, HEAD), bf16),
            pltpu.VMEM((n, PIECE, HEAD), bf16),
            pltpu.VMEM((n, PIECE, HEAD), bf16),
            pltpu.VMEM((8, n * rows), f32),
            pltpu.VMEM((8, n * cap_rows), f32),
            pltpu.VMEM((rows, width), bf16),
            pltpu.VMEM((rows, width), bf16),
            pltpu.VMEM((rows, width), bf16),
            pltpu.VMEM((sections, 2, cap_rows, width), bf16),
            pltpu.VMEM((2, cap_rows, width), bf16),
            pltpu.VMEM((rows, HEAD), f32),
            pltpu.VMEM((8, rows), f32),
            pltpu.VMEM((wides, 8, rows), f32),
            pltpu.VMEM((HEAD, rows), f32),
            dma((n, 6)), dma((n, 6)), dma((6,)),
            dma((n, 4)), dma((n, 4)), dma((4,)),
            dma((wides,)), dma((wides,)),
            dma((sections, 2)), dma((sections, 2)),
        ],
        compiler_params=pltpu.CompilerParams(
            collective_id=0, has_side_effects=True, vmem_limit_bytes=56 << 20
        ),
    )(counts, cap_len, owner, q, k, v, cq, cap, gq, gk, gcq, gck)


def per_device(
    q_self,
    k_self,
    v_self,
    gain_q_self,
    gain_k_self,
    counts,
    q_cross,
    cap_kv,
    gain_q_cross,
    gain_k_cross,
    cap_len,
    owner,
):
    out_self, out_cross = exchange_and_attend(
        counts, cap_len, owner,
        q_self[0], k_self[0], v_self[0], q_cross[0], cap_kv[:, 0],
        gain_q_self[None], gain_k_self[None], gain_q_cross[None], gain_k_cross[None],
    )
    return (out_self[None], out_cross[None])


def solution(mesh):
    whole = P("section", "seq", "wide")
    return jax.shard_map(
        per_device,
        mesh=mesh,
        in_specs=(
            whole, whole, whole, P("wide"), P("wide"), P(), whole,
            P(None, "section", "seq", "wide"), P("wide"), P("wide"), P(), P(),
        ),
        out_specs=(whole, whole),
        check_vma=False,
    )
```

```python
import functools
import math

import jax
import jax.numpy as jnp
from jax import lax
from jax.experimental import pallas as pl
from jax.experimental.pallas import tpu as pltpu
from jax.sharding import PartitionSpec as P

D = 5120
HEAD = 128
MESH = pl.DeviceIdType.MESH
MASKED = -1e30
PER_HEAD = 3
STEP = 80
PIECE = 96
EXTRA = PIECE - STEP


def square_sums(ref):
    floats = ref.astype(jnp.float32)
    return jnp.sum(floats * floats, axis=-1, keepdims=True)


def scaled_rows(values, factor, gain):
    return (values.astype(jnp.float32) * factor * gain).astype(jnp.bfloat16)


def attend(q, key_ref, value_ref, bias_ref, slots):
    total_slots, rows, _ = key_ref.shape
    block = slots * rows
    scale = math.log2(math.e) / math.sqrt(HEAD)

    def body(number, carry):
        top, total, accum = carry
        keys = key_ref[pl.ds(number * slots, slots)].reshape(block, HEAD)
        values = value_ref[pl.ds(number * slots, slots)].reshape(block, HEAD)
        scores = lax.dot_general(
            q, keys, (((1,), (1,)), ((), ())), preferred_element_type=jnp.float32
        )
        start = pl.multiple_of(number * block, 128)
        scores = scores + bias_ref[0:1, pl.ds(start, block)]
        newest = jnp.maximum(top, jnp.max(scores, axis=-1, keepdims=True))
        weights = jnp.exp2((scores - newest) * scale)
        rescale = jnp.exp2((top - newest) * scale)
        total = total * rescale + jnp.sum(weights, axis=-1, keepdims=True)
        accum = accum * rescale + jnp.dot(
            weights.astype(jnp.bfloat16), values, preferred_element_type=jnp.float32
        )
        return (newest, total, accum)

    count = q.shape[0]
    state = (
        jnp.full((count, 1), MASKED, jnp.float32),
        jnp.zeros((count, 1), jnp.float32),
        jnp.zeros((count, HEAD), jnp.float32),
    )
    top, total, accum = lax.fori_loop(0, total_slots // slots, body, state)
    return (accum / total).astype(jnp.bfloat16)


def main_kernel(
    n, sections, wides, heads_here,
    counts, cap_len, owner, q_raw, k_raw, v, cq_raw, cap, gq, gk, gcq, gck,
    out_self, out_cross,
    kr, vr, qr, ckr, cvr, cqr, os_buf, oc_buf, bias, cbias,
    q, k, cq, capr, chosen, columns_of, stat, stats, factors,
    send, recv, local, osend, orecv, olocal, wsend, wrecv, ssend, srecv,
):
    me = lax.axis_index("seq")
    section = lax.axis_index("section")
    wide = lax.axis_index("wide")
    owners = heads_here * PER_HEAD
    side = math.isqrt(n)

    def rank(index):
        return (index % side) * side + index // side if side * side == n else index

    mine = rank(me)
    third = mine % PER_HEAD
    barrier = pltpu.get_barrier_semaphore()
    for axis, here, size in (("seq", me, n), ("section", section, sections), ("wide", wide, wides)):
        @pl.loop(1, size)
        def _(d):
            pl.semaphore_signal(
                barrier, inc=1, device_id={axis: lax.rem(here + d, size)}, device_id_type=MESH
            )

    pl.semaphore_wait(barrier, n + sections + wides - 3)
    ck, cv = chosen.at[0], chosen.at[1]

    def pieces(target):
        columns = pl.ds(pl.multiple_of((rank(target) // PER_HEAD) * HEAD, HEAD), HEAD)
        part = pl.ds(pl.multiple_of((rank(target) % PER_HEAD) * STEP, 16), PIECE)
        return (
            (k.at[:, columns], kr),
            (v.at[:, columns], vr),
            (q.at[part, columns], qr),
            (ck.at[:, columns], ckr),
            (cv.at[:, columns], cvr),
            (cq.at[part, columns], cqr),
        )

    def copies(d, numbers=range(6)):
        target = lax.rem(me + d, n)
        return [
            pltpu.make_async_remote_copy(
                source, landing.at[me], send.at[d, number], recv.at[d, number],
                device_id={"seq": target}, device_id_type=MESH,
            )
            for number, (source, landing) in enumerate(pieces(target)) if number in numbers
        ]

    def own_copies(numbers=range(6)):
        return [
            pltpu.make_async_copy(source, landing.at[me], local.at[number])
            for number, (source, landing) in enumerate(pieces(me)) if number in numbers
        ]

    def start(numbers):
        @pl.loop(1, n)
        def _(d):
            @pl.when(rank(lax.rem(me + d, n)) < owners)
            def _():
                for copy in copies(d, numbers):
                    copy.start()

        @pl.when(mine < owners)
        def _():
            for copy in own_copies(numbers):
                copy.start()

    def to_section(d, number):
        return pltpu.make_async_remote_copy(
            (cap if number == 1 else capr.at[section]).at[number],
            capr.at[section, number], ssend.at[d, number], srecv.at[d, number],
            device_id={"section": lax.rem(section + d, sections)}, device_id_type=MESH,
        )

    def to_wide(d):
        return pltpu.make_async_remote_copy(
            stat, stats.at[wide], wsend.at[d], wrecv.at[d],
            device_id={"wide": lax.rem(wide + d, wides)}, device_id_type=MESH,
        )

    cap_rows = cap.shape[1]
    lane = lax.broadcasted_iota(jnp.int32, columns_of.shape, 1)
    columns_of[...] = jnp.where(
        lane == 0, square_sums(q_raw[...]),
        jnp.where(lane == 1, square_sums(k_raw[...]),
                  jnp.where(lane == 2, square_sums(cq_raw[...]), 0.0)),
    )
    columns_of[0:cap_rows] = jnp.where(
        lane[0:cap_rows] == 3, square_sums(cap[0]), columns_of[0:cap_rows]
    )
    partial = columns_of[...].T[0:8]
    stat[...] = partial
    stats[wide] = partial
    capr[section, 1] = cap[1]
    factors[...] = jnp.zeros(factors.shape, jnp.float32)

    @pl.loop(1, wides)
    def _(d):
        to_wide(d).start()

    start((1,))
    for d in range(1, sections):
        to_section(d, 1).start()

    source = section * 0
    for s in range(sections):
        source = jnp.where(owner[s] == section, s, source)
    position = lax.broadcasted_iota(jnp.int32, bias.shape, 1)
    bias[...] = jnp.where(position < counts[section], 0.0, MASKED)
    position = lax.broadcasted_iota(jnp.int32, cbias.shape, 1)
    cbias[...] = jnp.where(position < cap_len[source], 0.0, MASKED)

    @pl.loop(1, wides)
    def _(d):
        to_wide(d).wait_recv()

    total = stats[0]
    for w in range(1, wides):
        total = total + stats[w]
    factors[0:8] = lax.rsqrt(total / D + 1e-06)
    factor = factors[...].T
    capr[section, 0] = scaled_rows(cap[0], factor[0:cap_rows, 3:4], gck[...])
    k[...] = scaled_rows(k_raw[...], factor[:, 1:2], gk[...])
    q[...] = scaled_rows(q_raw[...], factor[:, 0:1], gq[...])
    cq[...] = scaled_rows(cq_raw[...], factor[:, 2:3], gcq[...])
    for d in range(1, sections):
        to_section(d, 0).start()
    start((0,))
    start((2, 5))
    for d in range(1, sections):
        for number in range(2):
            to_section(d, number).wait_recv()
    chosen[...] = capr[source]
    start((3, 4))

    def arrivals(d):
        for number, landing in enumerate((kr, vr, qr, ckr, cvr, cqr)):
            pltpu.make_async_remote_copy(
                landing.at[0], landing.at[0], send.at[d, number], recv.at[d, number],
                device_id={"seq": lax.rem(me + 1, n)}, device_id_type=MESH,
            ).wait_recv()

    columns = pl.ds(pl.multiple_of((mine // PER_HEAD) * HEAD, HEAD), HEAD)

    def results(d, to, make):
        rows = pl.ds(pl.multiple_of(third * STEP + EXTRA, 16), STEP)
        found = []
        for number, (buf, out) in enumerate(((os_buf, out_self), (oc_buf, out_cross))):
            found.append(
                make(buf.at[to, pl.ds(EXTRA, STEP)], out.at[rows, columns], d, 2 * number)
            )
        return found

    def first_rows(d, to, make):
        found = []
        for number, (buf, out) in enumerate(((os_buf, out_self), (oc_buf, out_cross))):
            found.append(
                make(buf.at[to, pl.ds(0, EXTRA)], out.at[pl.ds(0, EXTRA), columns], d, 2 * number + 1)
            )
        return found

    def remote(source, landing, d, number):
        return pltpu.make_async_remote_copy(
            source, landing, osend.at[d, number], orecv.at[d, number],
            device_id={"seq": lax.rem(me + d, n)}, device_id_type=MESH,
        )

    def nearby(source, landing, d, number):
        return pltpu.make_async_copy(source, landing, olocal.at[number])

    @pl.when(mine < owners)
    def _():
        for copy in own_copies():
            copy.wait()

        @pl.loop(1, n)
        def _(d):
            arrivals(d)

        group = 4

        def give(g):
            @pl.loop(0, group)
            def _(i):
                to = g * group + i
                d = lax.rem(to + n - me, n)
                for near, make in ((True, nearby), (False, remote)):
                    @pl.when((d == 0) if near else (d > 0))
                    def _():
                        for copy in results(d, to, make):
                            copy.start()

                        @pl.when(third == 0)
                        def _():
                            for copy in first_rows(d, to, make):
                                copy.start()

        @pl.loop(0, n // group)
        def _(g):
            queries = qr[pl.ds(g * group, group)].reshape(group * PIECE, HEAD)
            os_buf[pl.ds(g * group, group)] = attend(queries, kr, vr, bias, 4).reshape(
                group, PIECE, HEAD
            )
            queries = cqr[pl.ds(g * group, group)].reshape(group * PIECE, HEAD)
            oc_buf[pl.ds(g * group, group)] = attend(queries, ckr, cvr, cbias, 16).reshape(
                group, PIECE, HEAD
            )

            @pl.when(g > 0)
            def _():
                give(g - 1)


        give(n // group - 1)

    @pl.loop(1, n)
    def _(d):
        @pl.when(rank(lax.rem(me + d, n)) < owners)
        def _():
            for copy in copies(d):
                copy.wait_send()

        sender = lax.rem(me + n - d, n)
        for number, out in ((0, out_self), (2, out_cross)):
            @pl.when(rank(sender) < owners)
            def _():
                piece = out.at[pl.ds(0, STEP), pl.ds(0, HEAD)]
                remote(piece, piece, d, number).wait_recv()

            @pl.when((rank(sender) < owners) & (rank(sender) % PER_HEAD == 0))
            def _():
                piece = out.at[pl.ds(0, EXTRA), pl.ds(0, HEAD)]
                remote(piece, piece, d, number + 1).wait_recv()

    @pl.loop(1, wides)
    def _(d):
        to_wide(d).wait_send()

    for d in range(1, sections):
        for number in range(2):
            to_section(d, number).wait_send()

    @pl.when(mine < owners)
    def _():
        for copy in results(0, me, nearby):
            copy.wait()

        @pl.when(third == 0)
        def _():
            for copy in first_rows(0, me, nearby):
                copy.wait()

        @pl.loop(1, n)
        def _(d):
            for copy in results(d, lax.rem(me + d, n), remote):
                copy.wait_send()

            @pl.when(third == 0)
            def _():
                for copy in first_rows(d, lax.rem(me + d, n), remote):
                    copy.wait_send()


def exchange_and_attend(counts, cap_len, owner, q, k, v, cq, cap, gq, gk, gcq, gck):
    n, sections, wides = (lax.axis_size(axis) for axis in ("seq", "section", "wide"))
    rows, width = q.shape
    cap_rows = cap.shape[1]
    bf16, f32 = jnp.bfloat16, jnp.float32
    vmem = pl.BlockSpec(memory_space=pltpu.VMEM)
    dma = pltpu.SemaphoreType.DMA
    return pl.pallas_call(
        functools.partial(main_kernel, n, sections, wides, width // HEAD),
        out_shape=(
            jax.ShapeDtypeStruct((rows, width), bf16),
            jax.ShapeDtypeStruct((rows, width), bf16),
        ),
        in_specs=[pl.BlockSpec(memory_space=pltpu.SMEM)] * 3 + [vmem] * 9,
        out_specs=(vmem, vmem),
        scratch_shapes=[
            pltpu.VMEM((n, rows, HEAD), bf16),
            pltpu.VMEM((n, rows, HEAD), bf16),
            pltpu.VMEM((n, PIECE, HEAD), bf16),
            pltpu.VMEM((n, cap_rows, HEAD), bf16),
            pltpu.VMEM((n, cap_rows, HEAD), bf16),
            pltpu.VMEM((n, PIECE, HEAD), bf16),
            pltpu.VMEM((n, PIECE, HEAD), bf16),
            pltpu.VMEM((n, PIECE, HEAD), bf16),
            pltpu.VMEM((8, n * rows), f32),
            pltpu.VMEM((8, n * cap_rows), f32),
            pltpu.VMEM((rows, width), bf16),
            pltpu.VMEM((rows, width), bf16),
            pltpu.VMEM((rows, width), bf16),
            pltpu.VMEM((sections, 2, cap_rows, width), bf16),
            pltpu.VMEM((2, cap_rows, width), bf16),
            pltpu.VMEM((rows, HEAD), f32),
            pltpu.VMEM((8, rows), f32),
            pltpu.VMEM((wides, 8, rows), f32),
            pltpu.VMEM((HEAD, rows), f32),
            dma((n, 6)), dma((n, 6)), dma((6,)),
            dma((n, 4)), dma((n, 4)), dma((4,)),
            dma((wides,)), dma((wides,)),
            dma((sections, 2)), dma((sections, 2)),
        ],
        compiler_params=pltpu.CompilerParams(
            collective_id=0, has_side_effects=True, vmem_limit_bytes=56 << 20
        ),
    )(counts, cap_len, owner, q, k, v, cq, cap, gq, gk, gcq, gck)


def per_device(
    q_self,
    k_self,
    v_self,
    gain_q_self,
    gain_k_self,
    counts,
    q_cross,
    cap_kv,
    gain_q_cross,
    gain_k_cross,
    cap_len,
    owner,
):
    out_self, out_cross = exchange_and_attend(
        counts, cap_len, owner,
        q_self[0], k_self[0], v_self[0], q_cross[0], cap_kv[:, 0],
        gain_q_self[None], gain_k_self[None], gain_q_cross[None], gain_k_cross[None],
    )
    return (out_self[None], out_cross[None])


def solution(mesh):
    whole = P("section", "seq", "wide")
    return jax.shard_map(
        per_device,
        mesh=mesh,
        in_specs=(
            whole, whole, whole, P("wide"), P("wide"), P(), whole,
            P(None, "section", "seq", "wide"), P("wide"), P("wide"), P(), P(),
        ),
        out_specs=(whole, whole),
        check_vma=False,
    )
```

```python
import functools
import math

import jax
import jax.numpy as jnp
from jax import lax
from jax.experimental import pallas as pl
from jax.experimental.pallas import tpu as pltpu
from jax.sharding import PartitionSpec as P

D = 5120
HEAD = 128
MESH = pl.DeviceIdType.MESH
MASKED = -1e30
PER_HEAD = 3
STEP = 80
PIECE = 96
EXTRA = PIECE - STEP
GROUPS = 4


def square_sums(ref):
    floats = ref.astype(jnp.float32)
    return jnp.sum(floats * floats, axis=-1, keepdims=True)


def scaled_rows(values, factor, gain):
    return (values.astype(jnp.float32) * factor * gain).astype(jnp.bfloat16)


def first_state(state):
    top, total, accum = state
    top[...] = jnp.full(top.shape, MASKED, jnp.float32)
    total[...] = jnp.zeros(total.shape, jnp.float32)
    accum[...] = jnp.zeros(accum.shape, jnp.float32)


def attend(q_ref, keys, values, bias, state, after=None):
    scale = math.log2(math.e) / math.sqrt(HEAD)
    groups, count, _ = q_ref.shape
    top_ref, total_ref, accum_ref = state

    @pl.loop(0, groups)
    def _(g):
        scores = lax.dot_general(
            q_ref[g], keys, (((1,), (1,)), ((), ())), preferred_element_type=jnp.float32
        ) + bias
        top = top_ref[g][:, 0:1]
        newest = jnp.maximum(top, jnp.max(scores, axis=-1, keepdims=True))
        weights = jnp.exp2((scores - newest) * scale)
        rescale = jnp.exp2((top - newest) * scale)
        total = total_ref[g][:, 0:1] * rescale + jnp.sum(weights, axis=-1, keepdims=True)
        accum_ref[g] = accum_ref[g] * rescale + jnp.dot(
            weights.astype(jnp.bfloat16), values, preferred_element_type=jnp.float32
        )
        top_ref[g] = jnp.broadcast_to(newest, (count, HEAD))
        total_ref[g] = jnp.broadcast_to(total, (count, HEAD))
        if after is not None:
            after(g)


def main_kernel(
    n, sections, wides, heads_here,
    counts, cap_len, owner, q_raw, k_raw, v, cq_raw, cap, gq, gk, gcq, gck,
    out_self, out_cross,
    kr, vr, qr, ckr, cvr, cqr, os_buf, oc_buf, bias, cbias,
    q, k, cq, capr, chosen, columns_of, stat, stats, factors,
    queries, top_w, total_w, accum,
    send, recv, local, osend, orecv, olocal, wsend, wrecv, ssend, srecv,
):
    me = lax.axis_index("seq")
    section = lax.axis_index("section")
    wide = lax.axis_index("wide")
    owners = heads_here * PER_HEAD
    side = math.isqrt(n)

    def rank(index):
        return (index % side) * side + index // side if side * side == n else index

    mine = rank(me)
    third = mine % PER_HEAD
    barrier = pltpu.get_barrier_semaphore()
    for axis, here, size in (("seq", me, n), ("section", section, sections), ("wide", wide, wides)):
        @pl.loop(1, size)
        def _(d):
            pl.semaphore_signal(
                barrier, inc=1, device_id={axis: lax.rem(here + d, size)}, device_id_type=MESH
            )

    pl.semaphore_wait(barrier, n + sections + wides - 3)
    ck, cv = chosen.at[0], chosen.at[1]

    def pieces(target):
        columns = pl.ds(pl.multiple_of((rank(target) // PER_HEAD) * HEAD, HEAD), HEAD)
        part = pl.ds(pl.multiple_of((rank(target) % PER_HEAD) * STEP, 16), PIECE)
        return (
            (k.at[:, columns], kr),
            (v.at[:, columns], vr),
            (q.at[part, columns], qr),
            (ck.at[:, columns], ckr),
            (cv.at[:, columns], cvr),
            (cq.at[part, columns], cqr),
        )

    def copies(d, numbers=range(6)):
        target = lax.rem(me + d, n)
        return [
            pltpu.make_async_remote_copy(
                source, landing.at[d], send.at[d, number], recv.at[d, number],
                device_id={"seq": target}, device_id_type=MESH,
            )
            for number, (source, landing) in enumerate(pieces(target)) if number in numbers
        ]

    def own_copies(numbers=range(6)):
        return [
            pltpu.make_async_copy(source, landing.at[0], local.at[number])
            for number, (source, landing) in enumerate(pieces(me)) if number in numbers
        ]

    def start(numbers):
        @pl.loop(1, n)
        def _(d):
            @pl.when(rank(lax.rem(me + d, n)) < owners)
            def _():
                for copy in copies(d, numbers):
                    copy.start()

        @pl.when(mine < owners)
        def _():
            for copy in own_copies(numbers):
                copy.start()

    def to_section(d, number):
        return pltpu.make_async_remote_copy(
            (cap if number == 1 else capr.at[section]).at[number],
            capr.at[section, number], ssend.at[d, number], srecv.at[d, number],
            device_id={"section": lax.rem(section + d, sections)}, device_id_type=MESH,
        )

    def to_wide(d):
        return pltpu.make_async_remote_copy(
            stat, stats.at[wide], wsend.at[d], wrecv.at[d],
            device_id={"wide": lax.rem(wide + d, wides)}, device_id_type=MESH,
        )

    cap_rows = cap.shape[1]
    lane = lax.broadcasted_iota(jnp.int32, columns_of.shape, 1)
    columns_of[...] = jnp.where(
        lane == 0, square_sums(q_raw[...]),
        jnp.where(lane == 1, square_sums(k_raw[...]),
                  jnp.where(lane == 2, square_sums(cq_raw[...]), 0.0)),
    )
    columns_of[0:cap_rows] = jnp.where(
        lane[0:cap_rows] == 3, square_sums(cap[0]), columns_of[0:cap_rows]
    )
    partial = columns_of[...].T[0:8]
    stat[...] = partial
    stats[wide] = partial
    capr[section, 1] = cap[1]
    factors[...] = jnp.zeros(factors.shape, jnp.float32)

    @pl.loop(1, wides)
    def _(d):
        to_wide(d).start()

    start((1,))
    for d in range(1, sections):
        to_section(d, 1).start()

    source = section * 0
    for s in range(sections):
        source = jnp.where(owner[s] == section, s, source)
    for ref, limit in ((bias, counts[section]), (cbias, cap_len[source])):
        rows = ref.shape[1] // n
        lanes = lax.broadcasted_iota(jnp.int32, ref.shape, 1)
        step = me - lanes // rows
        position = jnp.where(step < 0, step + n, step) * rows + lanes % rows
        ref[...] = jnp.where(position < limit, 0.0, MASKED)

    @pl.loop(1, wides)
    def _(d):
        to_wide(d).wait_recv()

    total = stats[0]
    for w in range(1, wides):
        total = total + stats[w]
    factors[0:8] = lax.rsqrt(total / D + 1e-06)
    factor = factors[...].T
    capr[section, 0] = scaled_rows(cap[0], factor[0:cap_rows, 3:4], gck[...].reshape(1, -1))
    k[...] = scaled_rows(k_raw[...], factor[:, 1:2], gk[...].reshape(1, -1))
    q[...] = scaled_rows(q_raw[...], factor[:, 0:1], gq[...].reshape(1, -1))
    cq[...] = scaled_rows(cq_raw[...], factor[:, 2:3], gcq[...].reshape(1, -1))
    for d in range(1, sections):
        to_section(d, 0).start()
    start((5,))
    start((2,))
    for d in range(1, sections):
        for number in range(2):
            to_section(d, number).wait_recv()
    chosen[...] = capr[source]
    start((3, 4))
    start((0,))

    landings = (kr, vr, qr, ckr, cvr, cqr)

    def arrived(d, numbers):
        for number in numbers:
            landing = landings[number].at[0]
            pltpu.make_async_remote_copy(
                landing, landing, send.at[d, number], recv.at[d, number],
                device_id={"seq": lax.rem(me + 1, n)}, device_id_type=MESH,
            ).wait_recv()

    columns = pl.ds(pl.multiple_of((mine // PER_HEAD) * HEAD, HEAD), HEAD)

    def results(d, to, make, pairs=(0, 1)):
        rows = pl.ds(pl.multiple_of(third * STEP + EXTRA, 16), STEP)
        found = []
        for number, (buf, out) in enumerate(((os_buf, out_self), (oc_buf, out_cross))):
            if number in pairs:
                found.append(
                    make(buf.at[to, pl.ds(EXTRA, STEP)], out.at[rows, columns], d, 2 * number)
                )
        return found

    def first_rows(d, to, make, pairs=(0, 1)):
        found = []
        for number, (buf, out) in enumerate(((os_buf, out_self), (oc_buf, out_cross))):
            if number in pairs:
                landing = out.at[pl.ds(0, EXTRA), columns]
                found.append(make(buf.at[to, pl.ds(0, EXTRA)], landing, d, 2 * number + 1))
        return found

    def remote(source, landing, d, number):
        return pltpu.make_async_remote_copy(
            source, landing, osend.at[d, number], orecv.at[d, number],
            device_id={"seq": lax.rem(me + d, n)}, device_id_type=MESH,
        )

    def nearby(source, landing, d, number):
        return pltpu.make_async_copy(source, landing, olocal.at[number])

    @pl.when(mine < owners)
    def _():
        for copy in own_copies():
            copy.wait()

        def give(d, pairs):
            back = lax.rem(n - d, n)
            for near, make in ((True, nearby), (False, remote)):
                @pl.when((d == 0) if near else (d > 0))
                def _():
                    for copy in results(back, d, make, pairs):
                        copy.start()

                    @pl.when(third == 0)
                    def _():
                        for copy in first_rows(back, d, make, pairs):
                            copy.start()

        def finish(buf, pairs, g):
            buf[pl.ds(g * group, group)] = (accum[g] / total_w[g]).astype(
                jnp.bfloat16
            ).reshape(group, PIECE, HEAD)

            @pl.when(g > 0)
            def _():
                give_group(g - 1, pairs)

        def give_group(g, pairs):
            @pl.loop(0, group)
            def _(i):
                give(g * group + i, pairs)

        group = n // GROUPS
        state = (top_w, total_w, accum)

        @pl.loop(1, n)
        def _(d):
            arrived(d, (2, 3, 4, 5))

        @pl.loop(0, GROUPS)
        def _(g):
            queries[g] = cqr[pl.ds(g * group, group)].reshape(group * PIECE, HEAD)

        first_state(state)
        attend(
            queries, ckr[...].reshape(-1, HEAD), cvr[...].reshape(-1, HEAD), cbias[0:1], state,
            functools.partial(finish, oc_buf, (1,)),
        )

        @pl.loop(0, GROUPS)
        def _(g):
            queries[g] = qr[pl.ds(g * group, group)].reshape(group * PIECE, HEAD)

        first_state(state)

        give_group(GROUPS - 1, (1,))

        def self_block(b, after):
            @pl.loop(0, group)
            def _(i):
                @pl.when(b * group + i > 0)
                def _():
                    arrived(b * group + i, (1, 0))

            slots = pl.ds(b * group, group)
            block = group * kr.shape[1]
            attend(
                queries, kr[slots].reshape(block, HEAD), vr[slots].reshape(block, HEAD),
                bias[0:1, pl.ds(pl.multiple_of(b * block, HEAD), block)], state, after,
            )

        @pl.loop(0, GROUPS - 1)
        def _(b):
            self_block(b, None)

        self_block(GROUPS - 1, functools.partial(finish, os_buf, (0,)))
        give_group(GROUPS - 1, (0,))

    @pl.loop(1, n)
    def _(d):
        @pl.when(rank(lax.rem(me + d, n)) < owners)
        def _():
            for copy in copies(d):
                copy.wait_send()

        sender = lax.rem(me + n - d, n)
        for number, out in ((0, out_self), (2, out_cross)):
            @pl.when(rank(sender) < owners)
            def _():
                piece = out.at[pl.ds(0, STEP), pl.ds(0, HEAD)]
                remote(piece, piece, d, number).wait_recv()

            @pl.when((rank(sender) < owners) & (rank(sender) % PER_HEAD == 0))
            def _():
                piece = out.at[pl.ds(0, EXTRA), pl.ds(0, HEAD)]
                remote(piece, piece, d, number + 1).wait_recv()

    @pl.loop(1, wides)
    def _(d):
        to_wide(d).wait_send()

    for d in range(1, sections):
        for number in range(2):
            to_section(d, number).wait_send()

    @pl.when(mine < owners)
    def _():
        for copy in results(0, me, nearby):
            copy.wait()

        @pl.when(third == 0)
        def _():
            for copy in first_rows(0, me, nearby):
                copy.wait()

        @pl.loop(1, n)
        def _(d):
            for copy in results(d, lax.rem(me + d, n), remote):
                copy.wait_send()

            @pl.when(third == 0)
            def _():
                for copy in first_rows(d, lax.rem(me + d, n), remote):
                    copy.wait_send()


def exchange_and_attend(counts, cap_len, owner, q, k, v, cq, cap, gq, gk, gcq, gck):
    n, sections, wides = (lax.axis_size(axis) for axis in ("seq", "section", "wide"))
    rows, width = q.shape
    cap_rows = cap.shape[1]
    bf16, f32 = jnp.bfloat16, jnp.float32
    vmem = pl.BlockSpec(memory_space=pltpu.VMEM)
    dma = pltpu.SemaphoreType.DMA
    return pl.pallas_call(
        functools.partial(main_kernel, n, sections, wides, width // HEAD),
        out_shape=(
            jax.ShapeDtypeStruct((rows, width), bf16),
            jax.ShapeDtypeStruct((rows, width), bf16),
        ),
        in_specs=[pl.BlockSpec(memory_space=pltpu.SMEM)] * 3 + [vmem] * 9,
        out_specs=(vmem, vmem),
        scratch_shapes=[
            pltpu.VMEM((n, rows, HEAD), bf16),
            pltpu.VMEM((n, rows, HEAD), bf16),
            pltpu.VMEM((n, PIECE, HEAD), bf16),
            pltpu.VMEM((n, cap_rows, HEAD), bf16),
            pltpu.VMEM((n, cap_rows, HEAD), bf16),
            pltpu.VMEM((n, PIECE, HEAD), bf16),
            pltpu.VMEM((n, PIECE, HEAD), bf16),
            pltpu.VMEM((n, PIECE, HEAD), bf16),
            pltpu.VMEM((8, n * rows), f32),
            pltpu.VMEM((8, n * cap_rows), f32),
            pltpu.VMEM((rows, width), bf16),
            pltpu.VMEM((rows, width), bf16),
            pltpu.VMEM((rows, width), bf16),
            pltpu.VMEM((sections, 2, cap_rows, width), bf16),
            pltpu.VMEM((2, cap_rows, width), bf16),
            pltpu.VMEM((rows, HEAD), f32),
            pltpu.VMEM((8, rows), f32),
            pltpu.VMEM((wides, 8, rows), f32),
            pltpu.VMEM((HEAD, rows), f32),
            pltpu.VMEM((GROUPS, n // GROUPS * PIECE, HEAD), bf16),
            pltpu.VMEM((GROUPS, n // GROUPS * PIECE, HEAD), f32),
            pltpu.VMEM((GROUPS, n // GROUPS * PIECE, HEAD), f32),
            pltpu.VMEM((GROUPS, n // GROUPS * PIECE, HEAD), f32),
            dma((n, 6)), dma((n, 6)), dma((6,)),
            dma((n, 4)), dma((n, 4)), dma((4,)),
            dma((wides,)), dma((wides,)),
            dma((sections, 2)), dma((sections, 2)),
        ],
        compiler_params=pltpu.CompilerParams(
            collective_id=0, has_side_effects=True, vmem_limit_bytes=56 << 20
        ),
    )(counts, cap_len, owner, q, k, v, cq, cap, gq, gk, gcq, gck)


def per_device(
    q_self,
    k_self,
    v_self,
    gain_q_self,
    gain_k_self,
    counts,
    q_cross,
    cap_kv,
    gain_q_cross,
    gain_k_cross,
    cap_len,
    owner,
):
    out_self, out_cross = exchange_and_attend(
        counts, cap_len, owner,
        q_self[0], k_self[0], v_self[0], q_cross[0], cap_kv[:, 0],
        gain_q_self, gain_k_self, gain_q_cross, gain_k_cross,
    )
    return (out_self[None], out_cross[None])


def solution(mesh):
    whole = P("section", "seq", "wide")
    return jax.shard_map(
        per_device,
        mesh=mesh,
        in_specs=(
            whole, whole, whole, P("wide"), P("wide"), P(), whole,
            P(None, "section", "seq", "wide"), P("wide"), P("wide"), P(), P(),
        ),
        out_specs=(whole, whole),
        check_vma=False,
    )
```
